1024 devices in a mesh: dp: 16 (over z), rep: 16 (over x, y_lo, core), mp: 4 (over y_hi).
Axes of the slice: x: 4, y: 8 (y_hi: 4, y_lo: 2; y = y_hi * 2 + y_lo), z: 16, core: 2. Of those that a mesh axis runs over, the one named last changes fastest.
Arguments:
- kv_weight: bfloat16 [512, 128, 256], P(('dp', 'mp')), may hold values from -0.25 to 0.25
- queries: bfloat16 [16, 128, 192], P('rep', 'dp'), may hold values from -8 to 8, as said below
- kv_cache: bfloat16 [16, 4096, 576], P('rep', 'mp'), may hold values from -8 to 8, as said below
- lengths: int32 [16], P('rep'), may hold values from 1024 to 4096, as said below
Outputs:
- rollout_weight: bfloat16 [512, 128, 256], P(None, 'dp')
- attn_out: bfloat16 [16, 128, 128], P('rep', 'dp')
The draws below stay inside these ranges and needn't reach their ends.
Inputs may be any that keep to these rules, and one draw needn't show every extreme that they name: `lengths`: each request attends to cache positions 0 to its length - 1; some request has the full 4096. `queries`: entries are of order one. `kv_cache`: entries are of order one.
All inputs are finite; a program needn't handle non-finite values.
Results may differ from the reference program's by a relative error of at most 0.0072.
Values may be sent and summed in bfloat16 or wider, within the bound.
A program may use at most 32 MiB of HBM per device.

```python
import jax
import jax.numpy as jnp
from jax import lax

KVL = 512
HEADS = 128
NOPE = 128
ROPE = 64
VDIM = 128
ROWS = 16
LEN = 4096


def draw_queries(key, part):
    own = jax.random.fold_in(key, 1)
    values = jnp.clip(jax.random.normal(own, (ROWS, HEADS, NOPE + ROPE), jnp.float32), -8.0, 8.0)
    return values.astype(jnp.bfloat16)


def draw_kv_cache(key, part):
    own = jax.random.fold_in(key, 2)
    values = jnp.clip(jax.random.normal(own, (ROWS, LEN, KVL + ROPE), jnp.float32), -8.0, 8.0)
    return values.astype(jnp.bfloat16)


def draw_lengths(key, part):
    own = jax.random.fold_in(key, 3)
    values = jax.random.randint(own, (ROWS,), LEN // 4, LEN + 1, jnp.int32)
    return values.at[0].set(LEN)


def block_scale(stream_key, shape, pieces, low, largest):
    level = 1.0
    for axis_at, parts in pieces:
        steps = jax.random.uniform(jax.random.fold_in(jax.random.fold_in(stream_key, 6), axis_at), (parts,), jnp.float32, low / len(pieces), largest / len(pieces))
        level = level * jnp.repeat(jnp.exp(steps), shape[axis_at] // parts).reshape((-1,) + (1,) * (len(shape) - 1 - axis_at))
    return level


def centred(own_key, shape, width, limit, pieces=(), kind=jnp.bfloat16):
    values = width * jax.random.normal(own_key, shape, jnp.float32)
    if pieces:
        values = values * block_scale(own_key, shape, pieces, -0.22, 0.18)
    return jnp.clip(values, -limit, limit).astype(kind)


def setup_inputs(seed: int = 0) -> dict:
    splits = jax.random.split(jax.random.key(seed), 5)
    return {
        "kv_weight": centred(splits[0], (KVL, HEADS, NOPE + VDIM), KVL ** -0.5, 0.25, ((0, 64),)),
        "queries": draw_queries(jax.random.fold_in(splits[4], 71), 0),
        "kv_cache": draw_kv_cache(jax.random.fold_in(splits[4], 71), 0),
        "lengths": draw_lengths(jax.random.fold_in(splits[4], 71), 0),
    }


def reference(kv_weight, queries, kv_cache, lengths):
    key_weight = kv_weight[:, :, :NOPE]
    value_weight = kv_weight[:, :, NOPE:]
    absorbed = jnp.einsum("rhd,lhd->rhl", queries[:, :, :NOPE].astype(jnp.float32), key_weight.astype(jnp.float32)).astype(jnp.bfloat16)
    full_query = jnp.concatenate([absorbed, queries[:, :, NOPE:]], axis=-1)
    scale = (NOPE + ROPE) ** -0.5
    scores = jnp.einsum("rhc,rpc->rhp", full_query.astype(jnp.float32), kv_cache.astype(jnp.float32)) * scale
    positions = jnp.arange(LEN, dtype=jnp.int32)
    validity = positions[None, None, :] < lengths[:, None, None]
    masked = jnp.where(validity, scores, -1e30)
    top_score = jnp.max(masked, axis=-1, keepdims=True)
    expd = jnp.where(validity, jnp.exp(masked - top_score), 0.0)
    total_sum = jnp.sum(expd, axis=-1)
    soft_weights = expd.astype(jnp.bfloat16)
    latent = jnp.einsum("rhp,rpl->rhl", soft_weights.astype(jnp.float32), kv_cache[:, :, :KVL].astype(jnp.float32))
    latent = latent / total_sum[:, :, None]
    attn_out = jnp.einsum("rhl,lhv->rhv", latent, value_weight.astype(jnp.float32), precision=lax.Precision.HIGHEST)
    return kv_weight, attn_out.astype(jnp.bfloat16)
```

```python
import functools

import jax
import jax.numpy as jnp
from jax import lax
from jax.experimental import pallas as pl
from jax.experimental.pallas import tpu as pltpu
from jax.sharding import PartitionSpec as P

KVL = 512
NOPE = 128
ROPE = 64
VDIM = 128
WIDTH = NOPE + VDIM
NZ = 16
NY = 8
HPD = 8
MESH = pl.DeviceIdType.MESH

GROUPS = ((6, 11, 2.5), (4, 6, 4.2), (11, 13, 4.3), (13, 16, 7.4), (0, 4, 8.2))
HOP = 2.0


def spread(rows, cols, test):
    r = lax.broadcasted_iota(jnp.int32, (rows, cols), 0)
    c = lax.broadcasted_iota(jnp.int32, (rows, cols), 1)
    return jnp.where(test(r, c), 1.0, 0.0).astype(jnp.bfloat16)


def gather_kernel(
    kvw, qh, kth, lens, w, lat,
    share, relay, kt, qv, qall, ab_send, ab_recv, mg_send, mg_recv,
    loc_sem, z_send, z_recv, r_send, r_recv, f_send, q_send, q_recv,
    y_send, y_recv, c_send, c_recv, a_send, a_recv, m_send, m_recv,
):
    z = lax.axis_index("dp")
    k = lax.axis_index("rep")
    m = lax.axis_index("mp")
    x = k // 4
    ylo = (k // 2) % 2
    c = k % 2
    y = 2 * m + ylo
    s = 2 * ylo + c
    me = 2 * y + c
    sg = 1 - 2 * c

    def dev(zz, yy, cc):
        return {"dp": zz, "rep": x * 4 + (yy % 2) * 2 + cc, "mp": yy // 2}

    def zdev(d):
        return dev((z + d + NZ) % NZ, y, c)

    def remote(src, dst, send, recv, to):
        return pltpu.make_async_remote_copy(
            src_ref=src, dst_ref=dst, send_sem=send, recv_sem=recv, device_id=to, device_id_type=MESH
        )

    fetch_share = pltpu.make_async_copy(kvw.at[pl.ds(2 * s, 2)], share, loc_sem.at[0])
    fetch_kt = pltpu.make_async_copy(kth.at[0], kt, loc_sem.at[1])
    fetch_q = pltpu.make_async_copy(qh.at[0], qv, loc_sem.at[2])
    fetch_share.start()
    fetch_q.start()

    barrier = pltpu.get_barrier_semaphore()
    for d in (4, -4, 3, -3, 2, -2, 1, -1):
        pl.semaphore_signal(barrier, inc=1, device_id=zdev(d), device_id_type=MESH)
    for dy in range(NY):
        for dc in range(2):
            if dy or dc:
                to = dev(z, (y + dy) % NY, (c + dc) % 2)
                pl.semaphore_signal(barrier, inc=1, device_id=to, device_id_type=MESH)
    fetch_kt.start()
    fetch_share.wait()
    fetch_q.wait()
    own_q = pltpu.make_async_copy(qh.at[0, :, pl.ds(0, NOPE)], qall.at[s], loc_sem.at[3])
    own_q.start()
    own_w = pltpu.make_async_copy(share.at[:, z], w.at[8, y, c], loc_sem.at[4])
    own_w.start()
    pl.semaphore_wait(barrier, 8 + 15)

    started = []

    def piece(d):
        return share.at[:, (z + d + NZ) % NZ]

    far = [5, -5, 6, -6, 7, -7, 8]
    relays = {}
    for n, d in enumerate(far):
        step = 4 if d > 0 else -4
        cp = remote(piece(d), relay.at[n], r_send.at[n], r_recv.at[n], zdev(step))
        cp.start()
        relays[d] = cp
        started.append(cp)
    near = {}
    for n, d in enumerate((4, -4, 3, -3, 2, -2, 1, -1)):
        cp = remote(piece(d), w.at[8 - d, y, c], z_send.at[n], z_recv.at[8 - d], zdev(d))
        cp.start()
        near[d] = cp
        started.append(cp)

    q_in = []
    for n, (dl, dc) in enumerate(((0, 1), (1, 0), (1, 1))):
        to = dev(z, 2 * m + (ylo + dl) % 2, (c + dc) % 2)
        cp = remote(qv.at[:, pl.ds(0, NOPE)], qall.at[s], q_send.at[n], q_recv.at[n], to)
        cp.start()
        q_in.append(cp)
        started.append(cp)

    arrived = {}

    def z_wait(slot):
        if slot == 8:
            own_w.wait()
        elif 4 <= slot <= 12:
            near[8 - slot].wait_recv()
        else:
            forwards[8 - slot].wait_recv()

    forwards = {}

    def forward_far():
        for n, d in enumerate(far):
            relays[d].wait_recv()
            rest = d - 4 if d > 0 else d + 4
            cp = remote(relay.at[n], w.at[8 - d, y, c], f_send.at[n], z_recv.at[8 - d], zdev(rest))
            cp.start()
            forwards[d] = cp
            started.append(cp)

    core_in = []

    def to_core(g, src, n):
        lo, hi, _ = GROUPS[g]
        ref = w.at[pl.ds(lo, hi - lo), src, c]
        cp = remote(ref, ref, c_send.at[g, n], c_recv.at[g, n], dev(z, y, 1 - c))
        cp.start()
        core_in.append(cp)
        started.append(cp)

    def to_y(g, src, n, sign):
        lo, hi, _ = GROUPS[g]
        ref = w.at[pl.ds(lo, hi - lo), src, c]
        cp = remote(ref, ref, y_send.at[g, n], y_recv.at[g, n], dev(z, (y + sign * sg + NY) % NY, c))
        cp.start()
        arrived[g, n] = cp
        started.append(cp)

    def ready(g):
        lo, hi, _ = GROUPS[g]
        for slot in range(lo, hi):
            z_wait(slot)
        to_y(g, y, 0, 1)
        to_y(g, y, 4, -1)
        to_core(g, y, 0)

    def relay_y(g, step, sign):
        n = step - 1 if sign > 0 else 3 + step
        arrived[g, n].wait_recv()
        src = (y - sign * step * sg + 2 * NY) % NY
        if step < (4 if sign > 0 else 3):
            to_y(g, src, n + 1, sign)
        to_core(g, src, n + 1)

    def absorb():
        for cp in q_in:
            cp.wait_recv()
        own_q.wait()
        keys = w[:, y, c, :, :, 0:NOPE].astype(jnp.float32).reshape(2 * NZ * HPD, NOPE)
        ask = qall[...].astype(jnp.float32).reshape(4 * HPD, NOPE)
        cross = lax.dot_general(
            ask.astype(jnp.bfloat16), keys.astype(jnp.bfloat16), (((1,), (1,)), ((), ())),
            preferred_element_type=jnp.float32,
        )
        r = lax.broadcasted_iota(jnp.int32, cross.shape, 0)
        cc = lax.broadcasted_iota(jnp.int32, cross.shape, 1)
        own = jnp.where(r % HPD == cc % HPD, cross, 0.0).astype(jnp.bfloat16)
        base = 32 * (me % 4)
        pick = spread(2 * NZ * HPD, 128, lambda i, j: j == base + i // HPD)
        packed = jnp.dot(own, pick, preferred_element_type=jnp.float32)
        ab_send[...] = packed.reshape(4, HPD, 128).astype(jnp.bfloat16)
        for n in range(1, 16):
            dy, dc = n // 2, n % 2
            yy, cc2 = (y + dy) % NY, (c + dc) % 2
            cp = remote(
                ab_send.at[2 * (yy % 2) + cc2], ab_recv.at[me], a_send.at[n], a_recv.at[n], dev(z, yy, cc2)
            )
            cp.start()
            ab_in.append(cp)
            started.append(cp)
        own_ab = pltpu.make_async_copy(ab_send.at[s], ab_recv.at[me], loc_sem.at[5])
        own_ab.start()
        ab_own.append(own_ab)

    ab_in, ab_own, mg_in = [], [], []

    def attend():
        def place(i, j):
            src, slot, row = i // 32, (i % 32) // 2, i % 2
            return j == ((slot + z + 8) % NZ) * 32 + src * 2 + row

        perm = spread(KVL, KVL, place)
        fetch_kt.wait()
        ab_own[0].wait()
        for cp in ab_in:
            cp.wait_recv()
        tiles = [
            sum(ab_recv[4 * g + j].astype(jnp.float32) for j in range(4)) for g in range(4)
        ]
        got = jnp.concatenate(tiles, axis=1).astype(jnp.bfloat16)
        absorbed = jnp.dot(got, perm, preferred_element_type=jnp.float32).astype(jnp.bfloat16)
        scores = jnp.dot(absorbed, kt[0:KVL, :], preferred_element_type=jnp.float32)
        scores += jnp.dot(qv[:, NOPE : NOPE + ROPE], kt[KVL : KVL + ROPE, :], preferred_element_type=jnp.float32)
        scores = scores * ((NOPE + ROPE) ** (-0.5))
        count = kt.shape[1]
        positions = m * count + lax.broadcasted_iota(jnp.int32, scores.shape, 1)
        valid = positions < lens[0]
        masked = jnp.where(valid, scores, -1e30)
        top = jnp.max(masked, axis=1, keepdims=True)
        expd = jnp.where(valid, jnp.exp(masked - top), 0.0)
        total = jnp.sum(expd, axis=1, keepdims=True)
        part = lax.dot_general(
            expd.astype(jnp.bfloat16), kt[0:KVL, :], (((1,), (1,)), ((), ())),
            preferred_element_type=jnp.float32,
        )
        lane = lax.broadcasted_iota(jnp.int32, (HPD, 128), 1)
        mg_send[:, 0:KVL] = part
        mg_send[:, KVL : KVL + 128] = jnp.where(lane < 64, top, total)
        for n in range(1, 4):
            cp = remote(
                mg_send, mg_recv.at[n - 1], m_send.at[n], m_recv.at[n], dev(z, (y + 2 * n) % NY, c)
            )
            cp.start()
            mg_in.append(cp)
            started.append(cp)

    def merge():
        for cp in mg_in:
            cp.wait_recv()
        parts = [mg_send[...]] + [mg_recv[n] for n in range(3)]
        tops = [p[:, KVL : KVL + 1] for p in parts]
        totals = [p[:, KVL + 64 : KVL + 65] for p in parts]
        top = jnp.maximum(jnp.maximum(tops[0], tops[1]), jnp.maximum(tops[2], tops[3]))
        factors = [jnp.exp(t - top) for t in tops]
        total = sum(f * t for f, t in zip(factors, totals))
        value = sum(f * p[:, 0:KVL] for f, p in zip(factors, parts))
        lat[...] = value / total

    events = [(3.9, forward_far), (8.7, absorb), (13.5, attend), (19.0, merge)]
    for g, (_, _, at) in enumerate(GROUPS):
        events.append((at, functools.partial(ready, g)))
        for step in range(1, 5):
            events.append((at + step * HOP, functools.partial(relay_y, g, step, 1)))
            if step < 4:
                events.append((at + step * HOP, functools.partial(relay_y, g, step, -1)))
    events.sort(key=lambda e: e[0])
    for _, run in events:
        run()
    for cp in core_in:
        cp.wait_recv()
    for cp in started:
        cp.wait_send()


def project_kernel(w, lat, out, attn, sems):
    z = lax.axis_index("dp")
    copies = []
    for i in range(NZ):
        slot = (i - z + 8 + NZ) % NZ
        cp = pltpu.make_async_copy(w.at[slot], out.at[i], sems.at[i])
        cp.start()
        copies.append(cp)
    value = lat[...]
    high = value.astype(jnp.bfloat16)
    low = (value - high.astype(jnp.float32)).astype(jnp.bfloat16)
    both = jnp.concatenate([high.astype(jnp.float32), low.astype(jnp.float32)], axis=0).astype(jnp.bfloat16)
    widen = spread(128, 128 * HPD, lambda i, j: j // HPD == i)
    r = lax.broadcasted_iota(jnp.int32, (2 * HPD, 128 * HPD), 0)
    cc = lax.broadcasted_iota(jnp.int32, (2 * HPD, 128 * HPD), 1)
    diagonal = r % HPD == cc % HPD
    total = jnp.zeros((2 * HPD, VDIM), jnp.float32)
    for g in range(4):
        wide = jnp.dot(both[:, g * 128 : (g + 1) * 128], widen, preferred_element_type=jnp.float32)
        wide = jnp.where(diagonal, wide, 0.0).astype(jnp.bfloat16)
        for j in range(4):
            slot = (4 * g + j - z + 8 + NZ) % NZ
            vals = w[slot, :, :, :, :, NOPE:WIDTH].astype(jnp.float32).reshape(32 * HPD, VDIM)
            total += jnp.dot(
                wide[:, j * 256 : (j + 1) * 256], vals.astype(jnp.bfloat16), preferred_element_type=jnp.float32
            )
    attn[0] = (total[0:HPD] + total[HPD:]).astype(jnp.bfloat16)
    for cp in copies:
        cp.wait()


def per_device(kv_weight, queries, kv_cache, lengths):
    rows = kv_weight.shape[0]
    kvw = kv_weight.reshape(rows, NZ, HPD, WIDTH)
    kth = jnp.swapaxes(kv_cache, 1, 2)
    count = kth.shape[2]
    dma = pltpu.SemaphoreType.DMA
    groups = len(GROUPS)
    vmem = pl.BlockSpec(memory_space=pltpu.VMEM)
    hbm = pl.BlockSpec(memory_space=pl.ANY)
    w_shape = jax.ShapeDtypeStruct((NZ, NY, 2, 2, HPD, WIDTH), jnp.bfloat16)
    w, lat = pl.pallas_call(
        gather_kernel,
        out_shape=(w_shape, jax.ShapeDtypeStruct((HPD, KVL), jnp.float32)),
        in_specs=[hbm, hbm, hbm, pl.BlockSpec(memory_space=pltpu.SMEM)],
        out_specs=(vmem, vmem),
        scratch_shapes=[
            pltpu.VMEM((2, NZ, HPD, WIDTH), jnp.bfloat16),
            pltpu.VMEM((7, 2, HPD, WIDTH), jnp.bfloat16),
            pltpu.VMEM((KVL + ROPE, count), jnp.bfloat16),
            pltpu.VMEM((HPD, NOPE + ROPE), jnp.bfloat16),
            pltpu.VMEM((4, HPD, NOPE), jnp.bfloat16),
            pltpu.VMEM((4, HPD, 128), jnp.bfloat16),
            pltpu.VMEM((16, HPD, 128), jnp.bfloat16),
            pltpu.VMEM((HPD, KVL + 128), jnp.float32),
            pltpu.VMEM((3, HPD, KVL + 128), jnp.float32),
            dma((6,)), dma((8,)), dma((16,)), dma((7,)), dma((7,)), dma((7,)), dma((3,)), dma((3,)),
            dma((groups, 7)), dma((groups, 7)), dma((groups, 8)), dma((groups, 8)),
            dma((16,)), dma((16,)), dma((4,)), dma((4,)),
        ],
        compiler_params=pltpu.CompilerParams(collective_id=0, has_side_effects=True),
        name="gather",
    )(kvw, queries, kth, lengths)
    out, attn = pl.pallas_call(
        project_kernel,
        out_shape=(w_shape, jax.ShapeDtypeStruct((1, HPD, VDIM), jnp.bfloat16)),
        in_specs=[vmem, vmem],
        out_specs=(hbm, vmem),
        scratch_shapes=[dma((NZ,))],
        name="project",
    )(w, lat)
    return out.reshape(KVL, HPD, WIDTH), attn


def solution(mesh):
    in_specs = (P(("dp", "mp"), None, None), P("rep", "dp", None), P("rep", "mp", None), P("rep"))
    out_specs = (P(None, "dp", None), P("rep", "dp", None))
    return jax.shard_map(per_device, mesh=mesh, in_specs=in_specs, out_specs=out_specs, check_vma=False)
```

```python
import functools

import jax
import jax.numpy as jnp
from jax import lax
from jax.experimental import pallas as pl
from jax.experimental.pallas import tpu as pltpu
from jax.sharding import PartitionSpec as P

KVL = 512
NOPE = 128
ROPE = 64
VDIM = 128
WIDTH = NOPE + VDIM
NX = 4
NY = 8
NZ = 16
HPD = 8
MESH = pl.DeviceIdType.MESH

NEAR, FAR = 0, 1
REACH = (4, -4, 3, -3, 2, -2, 1, -1)
FAR_D = (8, 7, -7, 6, -6, 5, -5)


def spread(rows, cols, test):
    r = lax.broadcasted_iota(jnp.int32, (rows, cols), 0)
    c = lax.broadcasted_iota(jnp.int32, (rows, cols), 1)
    return jnp.where(test(r, c), 1.0, 0.0).astype(jnp.bfloat16)


def gather_kernel(
    kvw, qh, kth, lenh, w, lat,
    share, zkeys, relay_k, relay_v, kt, qv, lens, qall, ab_send, ab_recv, mg_send, mg_recv,
    loc, zs, zn, zr, zf, fs, vs, vr, vq, qs, qr, ys, yr, xs, xf, xb, xq, cs, cr, a_s, a_r, m_s, m_r,
):
    z = lax.axis_index("dp")
    k = lax.axis_index("rep")
    m = lax.axis_index("mp")
    x = k // 4
    ylo = (k // 2) % 2
    c = k % 2
    y = 2 * m + ylo
    s = 2 * ylo + c
    me = 2 * y + c
    sg = 1 - 2 * c
    key = pl.ds(0, NOPE)
    pair = pl.ds(2 * c, 2)

    def dev(zz, yy, cc, xx=x):
        return {"dp": zz, "rep": xx * 4 + (yy % 2) * 2 + cc, "mp": yy // 2}

    def zdev(d):
        return dev((z + d + 2 * NZ) % NZ, y, c)

    def xdev(d):
        return dev(z, y, c, (x + d + NX) % NX)

    def remote(src, dst, send, recv, to):
        return pltpu.make_async_remote_copy(
            src_ref=src, dst_ref=dst, send_sem=send, recv_sem=recv, device_id=to, device_id_type=MESH
        )

    def local(src, dst, sem):
        return pltpu.make_async_copy(src, dst, sem)

    def wait_all(sem, ref):
        local(ref, ref, sem).wait()

    fetch_w = local(kvw.at[pl.ds(2 * s, 2)], share, loc.at[0])
    fetch_kt = local(kth.at[0], kt, loc.at[1])
    fetch_q = local(qh.at[0], qv, loc.at[2])
    fetch_l = local(lenh, lens, loc.at[3])
    fetch_w.start()
    fetch_q.start()

    barrier = pltpu.get_barrier_semaphore()
    for d in REACH:
        pl.semaphore_signal(barrier, inc=1, device_id=zdev(d), device_id_type=MESH)
    for n in range(1, 2 * NY):
        to = dev(z, (y + n // 2) % NY, (c + n % 2) % 2)
        pl.semaphore_signal(barrier, inc=1, device_id=to, device_id_type=MESH)
    for d in (1, -1):
        pl.semaphore_signal(barrier, inc=1, device_id=xdev(d), device_id_type=MESH)
    fetch_kt.start()
    fetch_l.start()
    fetch_w.wait()
    fetch_q.wait()
    own_q = local(qh.at[0, :, pl.ds(0, NOPE)], qall.at[s], loc.at[4])
    own_q.start()
    own_k = local(share.at[:, z, :, key], zkeys.at[4], loc.at[5])
    own_k.start()
    pl.semaphore_wait(barrier, len(REACH) + 15 + 2)

    def piece(d):
        return share.at[:, (z + d + 2 * NZ) % NZ]

    def key_piece(d):
        return share.at[:, (z + d + 2 * NZ) % NZ, :, key]

    for n, d in enumerate(FAR_D):
        remote(key_piece(d), relay_k.at[n], zs, zr, zdev(4 if d > 0 else -4)).start()
    for d in REACH:
        remote(key_piece(d), zkeys.at[(4 - d) % NZ], zs, zn, zdev(d)).start()
    up = remote(piece(8 - x), relay_v.at[1], vs.at[3], vq.at[1], zdev(4))
    down = remote(piece(-4 - x), relay_v.at[0], vs.at[2], vq.at[0], zdev(-4))
    ahead = remote(piece(4 - x), w.at[0, x, y, pair], vs.at[0], vr.at[0], zdev(4 - x))
    behind = remote(piece(-x), w.at[1, x, y, pair], vs.at[1], vr.at[1], zdev(-x))
    behind_own = local(piece(0), w.at[1, x, y, pair], vr.at[1])
    up.start()
    down.start()
    ahead.start()

    @pl.when(x > 0)
    def _():
        behind.start()

    @pl.when(x == 0)
    def _():
        behind_own.start()

    for dl, dc in ((0, 1), (1, 0), (1, 1)):
        to = dev(z, 2 * m + (ylo + dl) % 2, (c + dc) % 2)
        remote(qv.at[:, pl.ds(0, NOPE)], qall.at[s], qs, qr, to).start()

    up_rest = remote(relay_v.at[1], w.at[3, x, y, pair], vs.at[5], vr.at[3], zdev(4 - x))
    down_rest = remote(relay_v.at[0], w.at[2, x, y, pair], vs.at[4], vr.at[2], zdev(-x))
    down_own = local(relay_v.at[0], w.at[2, x, y, pair], vr.at[2])

    def forward_far():
        wait_all(zr, relay_k)
        for n, d in enumerate(FAR_D):
            rest = d - 4 if d > 0 else d + 4
            remote(relay_k.at[n], zkeys.at[(4 - d) % NZ], fs, zf, zdev(rest)).start()
        up.wait_recv()
        up_rest.start()
        down.wait_recv()

        @pl.when(x > 0)
        def _():
            down_rest.start()

        @pl.when(x == 0)
        def _():
            down_own.start()

    def chunk(g, src):
        return w.at[pl.ds(2 * g, 2), x, src, pair]

    def to_y(g):
        for n in (4, 3, 5, 2, 6, 1, 7):
            remote(chunk(g, y), chunk(g, y), ys.at[g], yr.at[g], dev(z, (y + n) % NY, c)).start()

    def near_ready():
        wait_all(zn, zkeys.at[pl.ds(0, 8)])
        own_k.wait()
        ahead.wait_recv()
        behind.wait_recv()
        to_y(NEAR)

    def far_keys():
        wait_all(zf, relay_k)

    def far_ready():
        up_rest.wait_recv()
        down_rest.wait_recv()
        to_y(FAR)

    def part(g, n, b):
        return w.at[2 * g + n // 2, b, pl.ds(4 * (n % 2), 4), pair]

    def to_x(g):
        wait_all(yr.at[g], w.at[0, 0, pl.ds(0, 7)])
        for n in range(4):
            ref = part(g, n, x)
            remote(ref, ref, xs.at[g], xf.at[g, n], xdev(sg)).start()
            remote(ref, ref, xs.at[g], xb.at[g], xdev(-sg)).start()
        to_core(g, x)

    def relay_x(g, n):
        ref = part(g, n, (x - sg + NX) % NX)
        cp = remote(ref, ref, xs.at[g], xf.at[g, n], xdev(sg))
        cp.wait_recv()
        remote(ref, ref, xs.at[g], xq.at[g], xdev(sg)).start()

    def to_core(g, b):
        ref = w.at[pl.ds(2 * g, 2), b, :, pair]
        remote(ref, ref, cs, cr, dev(z, y, 1 - c)).start()

    def behind_x(g):
        to_core(g, (x - sg + NX) % NX)

    def other_x(g):
        wait_all(xb.at[g], w.at[0, 0])
        to_core(g, (x + sg + NX) % NX)

    def across_x(g):
        wait_all(xq.at[g], w.at[0, 0])
        to_core(g, (x + 2) % NX)

    def absorb():
        wait_all(qr, qall.at[pl.ds(0, 3)])
        own_q.wait()
        keys = zkeys[...].astype(jnp.float32).reshape(2 * NZ * HPD, NOPE)
        ask = qall[...].astype(jnp.float32).reshape(4 * HPD, NOPE)
        cross = lax.dot_general(
            ask.astype(jnp.bfloat16), keys.astype(jnp.bfloat16), (((1,), (1,)), ((), ())),
            preferred_element_type=jnp.float32,
        )
        r = lax.broadcasted_iota(jnp.int32, cross.shape, 0)
        cc = lax.broadcasted_iota(jnp.int32, cross.shape, 1)
        own = jnp.where(r % HPD == cc % HPD, cross, 0.0).astype(jnp.bfloat16)
        base = 32 * (me % 4)
        pick = spread(2 * NZ * HPD, 128, lambda i, j: j == base + i // HPD)
        packed = jnp.dot(own, pick, preferred_element_type=jnp.float32)
        ab_send[...] = packed.reshape(4, HPD, 128).astype(jnp.bfloat16)
        own_ab.start()
        for n in (8, 9, 7, 10, 6, 11, 5, 12, 4, 13, 3, 14, 2, 15, 1):
            yy, cc2 = (y + n // 2) % NY, (c + n % 2) % 2
            remote(ab_send.at[2 * (yy % 2) + cc2], ab_recv.at[me], a_s, a_r, dev(z, yy, cc2)).start()

    own_ab = local(ab_send.at[s], ab_recv.at[me], loc.at[6])

    def attend():
        def place(i, j):
            src, slot, row = i // 32, (i % 32) // 2, i % 2
            return j == ((slot + z + 12) % NZ) * 32 + src * 2 + row

        perm = spread(KVL, KVL, place)
        fetch_kt.wait()
        fetch_l.wait()
        own_ab.wait()
        wait_all(a_r, ab_recv.at[pl.ds(0, 15)])
        tiles = [sum(ab_recv[4 * g + j].astype(jnp.float32) for j in range(4)) for g in range(4)]
        got = jnp.concatenate(tiles, axis=1).astype(jnp.bfloat16)
        absorbed = jnp.dot(got, perm, preferred_element_type=jnp.float32).astype(jnp.bfloat16)
        scores = jnp.dot(absorbed, kt[0:KVL, :], preferred_element_type=jnp.float32)
        scores += jnp.dot(qv[:, NOPE : NOPE + ROPE], kt[KVL : KVL + ROPE, :], preferred_element_type=jnp.float32)
        scores = scores * ((NOPE + ROPE) ** (-0.5))
        count = kt.shape[1]
        positions = m * count + lax.broadcasted_iota(jnp.int32, scores.shape, 1)
        valid = positions < lens[0]
        masked = jnp.where(valid, scores, -1e30)
        top = jnp.max(masked, axis=1, keepdims=True)
        expd = jnp.where(valid, jnp.exp(masked - top), 0.0)
        total = jnp.sum(expd, axis=1, keepdims=True)
        part = lax.dot_general(
            expd.astype(jnp.bfloat16), kt[0:KVL, :], (((1,), (1,)), ((), ())),
            preferred_element_type=jnp.float32,
        )
        lane = lax.broadcasted_iota(jnp.int32, (HPD, 128), 1)
        mg_send[:, 0:KVL] = part
        mg_send[:, KVL : KVL + 128] = jnp.where(lane < 64, top, total)
        for n in (2, 1, 3):
            to = dev(z, (y + 2 * n) % NY, c)
            remote(mg_send, mg_recv.at[n - 1], m_s, m_r, to).start()

    def merge():
        wait_all(m_r, mg_recv)
        parts = [mg_send[...]] + [mg_recv[n] for n in range(3)]
        tops = [p[:, KVL : KVL + 1] for p in parts]
        totals = [p[:, KVL + 64 : KVL + 65] for p in parts]
        top = jnp.maximum(jnp.maximum(tops[0], tops[1]), jnp.maximum(tops[2], tops[3]))
        factors = [jnp.exp(t - top) for t in tops]
        total = sum(f * t for f, t in zip(factors, totals))
        value = sum(f * p[:, 0:KVL] for f, p in zip(factors, parts))
        lat[...] = value / total

    forward_far()
    near_ready()
    far_keys()
    far_ready()
    absorb()
    to_x(NEAR)
    for n in range(4):
        relay_x(NEAR, n)
    attend()
    to_x(FAR)
    behind_x(NEAR)
    other_x(NEAR)
    across_x(NEAR)
    for n in range(4):
        relay_x(FAR, n)
    behind_x(FAR)
    other_x(FAR)
    merge()
    across_x(FAR)
    wait_all(cr, w.at[pl.ds(0, 2)])

    wait_all(zs, zkeys.at[pl.ds(0, 15)])
    wait_all(fs, relay_k)
    for cp in (up, down, ahead, up_rest):
        cp.wait_send()

    @pl.when(x > 0)
    def _():
        behind.wait_send()
        down_rest.wait_send()

    wait_all(qs, qall.at[pl.ds(0, 3)])
    for g in (NEAR, FAR):
        wait_all(ys.at[g], w.at[0, 0, pl.ds(0, 7)])
        wait_all(xs.at[g], w.at[0, pl.ds(0, 3)])
    wait_all(cs, w.at[pl.ds(0, 2)])
    wait_all(a_s, ab_recv.at[pl.ds(0, 15)])
    wait_all(m_s, mg_recv)


def project_kernel(w, lat, out, attn, sems):
    z = lax.axis_index("dp")
    copies = []
    for i in range(NZ):
        slot = (i - z + 4 + NZ) % NZ
        cp = pltpu.make_async_copy(w.at[slot // 4, slot % 4], out.at[i], sems.at[i])
        cp.start()
        copies.append(cp)
    value = lat[...]
    high = value.astype(jnp.bfloat16).astype(jnp.float32)
    both = jnp.concatenate([high, value - high], axis=0).astype(jnp.bfloat16)
    widen = spread(128, 128 * HPD, lambda i, j: j // HPD == i)
    r = lax.broadcasted_iota(jnp.int32, (2 * HPD, 128 * HPD), 0)
    cc = lax.broadcasted_iota(jnp.int32, (2 * HPD, 128 * HPD), 1)
    diagonal = r % HPD == cc % HPD
    total = jnp.zeros((2 * HPD, VDIM), jnp.float32)
    for g in range(4):
        wide = jnp.dot(both[:, g * 128 : (g + 1) * 128], widen, preferred_element_type=jnp.float32)
        wide = jnp.where(diagonal, wide, 0.0).astype(jnp.bfloat16)
        for j in range(4):
            slot = (4 * g + j - z + 4 + NZ) % NZ
            vals = w[slot // 4, slot % 4, :, :, :, NOPE:WIDTH].astype(jnp.float32).reshape(32 * HPD, VDIM)
            total += jnp.dot(
                wide[:, j * 256 : (j + 1) * 256], vals.astype(jnp.bfloat16), preferred_element_type=jnp.float32
            )
    attn[0] = (total[0:HPD] + total[HPD:]).astype(jnp.bfloat16)
    for cp in copies:
        cp.wait()


def per_device(kv_weight, queries, kv_cache, lengths):
    rows = kv_weight.shape[0]
    kvw = kv_weight.reshape(rows, NZ, HPD, WIDTH)
    kth = jnp.swapaxes(kv_cache, 1, 2)
    count = kth.shape[2]
    dma = pltpu.SemaphoreType.DMA
    bf16, f32 = jnp.bfloat16, jnp.float32
    vmem = pl.BlockSpec(memory_space=pltpu.VMEM)
    hbm = pl.BlockSpec(memory_space=pltpu.HBM)
    shape = (4, 4, NY, 4, HPD, WIDTH)
    w, lat = pl.pallas_call(
        gather_kernel,
        out_shape=(pltpu.VMEM(shape, bf16), pltpu.VMEM((HPD, KVL), f32)),
        in_specs=[hbm, hbm, hbm, hbm],
        out_specs=(vmem, vmem),
        scratch_shapes=[
            pltpu.VMEM((2, NZ, HPD, WIDTH), bf16),
            pltpu.VMEM((NZ, 2, HPD, NOPE), bf16),
            pltpu.VMEM((7, 2, HPD, NOPE), bf16),
            pltpu.VMEM((2, 2, HPD, WIDTH), bf16),
            pltpu.VMEM((KVL + ROPE, count), bf16),
            pltpu.VMEM((HPD, NOPE + ROPE), bf16),
            pltpu.SMEM((1,), jnp.int32),
            pltpu.VMEM((4, HPD, NOPE), bf16),
            pltpu.VMEM((4, HPD, 128), bf16),
            pltpu.VMEM((16, HPD, 128), bf16),
            pltpu.VMEM((HPD, KVL + 128), f32),
            pltpu.VMEM((3, HPD, KVL + 128), f32),
            dma((7,)), dma, dma, dma, dma, dma, dma((6,)), dma((4,)), dma((2,)), dma, dma,
            dma((2,)), dma((2,)), dma((2,)), dma((2, 4)), dma((2,)), dma((2,)), dma, dma, dma, dma, dma, dma,
        ],
        compiler_params=pltpu.CompilerParams(collective_id=0, has_side_effects=True),
        name="gather",
    )(kvw, queries, kth, lengths)
    w = pltpu.with_memory_space_constraint(w, pltpu.VMEM)
    lat = pltpu.with_memory_space_constraint(lat, pltpu.VMEM)
    out, attn = pl.pallas_call(
        project_kernel,
        out_shape=(jax.ShapeDtypeStruct((NZ, NY, 4, HPD, WIDTH), bf16), jax.ShapeDtypeStruct((1, HPD, VDIM), bf16)),
        in_specs=[vmem, vmem],
        out_specs=(hbm, vmem),
        scratch_shapes=[dma((NZ,))],
        name="project",
    )(w, lat)
    return out.reshape(KVL, HPD, WIDTH), attn


def solution(mesh):
    in_specs = (P(("dp", "mp"), None, None), P("rep", "dp", None), P("rep", "mp", None), P("rep"))
    out_specs = (P(None, "dp", None), P("rep", "dp", None))
    return jax.shard_map(per_device, mesh=mesh, in_specs=in_specs, out_specs=out_specs, check_vma=False)
```

```python
import functools

import jax
import jax.numpy as jnp
from jax import lax
from jax.experimental import pallas as pl
from jax.experimental.pallas import tpu as pltpu
from jax.sharding import PartitionSpec as P

KVL = 512
NOPE = 128
ROPE = 64
VDIM = 128
WIDTH = NOPE + VDIM
NX = 4
NY = 8
NZ = 16
HPD = 8
MESH = pl.DeviceIdType.MESH

NEAR, FAR = 0, 1
REACH = (4, -4, 3, -3, 2, -2, 1, -1)
FAR_D = (8, 7, -7, 6, -6, 5, -5)


def spread(rows, cols, test):
    r = lax.broadcasted_iota(jnp.int32, (rows, cols), 0)
    c = lax.broadcasted_iota(jnp.int32, (rows, cols), 1)
    return jnp.where(test(r, c), 1.0, 0.0).astype(jnp.bfloat16)


def gather_kernel(
    kvw, qh, kth, lenh, w, wide,
    perm, pick, widen, share, zkeys, relay_k, relay_v, kt, qv, lens, qall, ab_send, ab_recv, mg_send, mg_recv,
    loc, zs, zn, zr, zf, fs, vs, vr, vq, qs, qr, ys, yr, xs, xf, xb, xq, cs, cr, a_s, a_r, m_s, m_r,
):
    z = lax.axis_index("dp")
    k = lax.axis_index("rep")
    m = lax.axis_index("mp")
    x = k // 4
    ylo = (k // 2) % 2
    c = k % 2
    y = 2 * m + ylo
    s = 2 * ylo + c
    me = 2 * y + c
    sg = 1 - 2 * c
    key = pl.ds(0, NOPE)
    pair = pl.ds(2 * c, 2)

    def dev(zz, yy, cc, xx=x):
        return {"dp": zz, "rep": xx * 4 + (yy % 2) * 2 + cc, "mp": yy // 2}

    def zdev(d):
        return dev((z + d + 2 * NZ) % NZ, y, c)

    def xdev(d):
        return dev(z, y, c, (x + d + NX) % NX)

    def remote(src, dst, send, recv, to):
        return pltpu.make_async_remote_copy(
            src_ref=src, dst_ref=dst, send_sem=send, recv_sem=recv, device_id=to, device_id_type=MESH
        )

    def local(src, dst, sem):
        return pltpu.make_async_copy(src, dst, sem)

    def wait_all(sem, ref):
        local(ref, ref, sem).wait()

    fetch_w = local(kvw.at[pl.ds(2 * s, 2)], share, loc.at[0])
    fetch_kt = local(kth.at[0], kt, loc.at[1])
    fetch_q = local(qh.at[0], qv, loc.at[2])
    fetch_l = local(lenh, lens, loc.at[3])
    fetch_w.start()
    fetch_q.start()

    barrier = pltpu.get_barrier_semaphore()
    for d in REACH:
        pl.semaphore_signal(barrier, inc=1, device_id=zdev(d), device_id_type=MESH)
    for n in range(1, 2 * NY):
        to = dev(z, (y + n // 2) % NY, (c + n % 2) % 2)
        pl.semaphore_signal(barrier, inc=1, device_id=to, device_id_type=MESH)
    for d in (1, -1):
        pl.semaphore_signal(barrier, inc=1, device_id=xdev(d), device_id_type=MESH)
    fetch_kt.start()
    fetch_l.start()
    fetch_w.wait()
    fetch_q.wait()
    own_q = local(qh.at[0, :, pl.ds(0, NOPE)], qall.at[s], loc.at[4])
    own_q.start()
    own_k = local(share.at[:, z, :, key], zkeys.at[4], loc.at[5])
    own_k.start()

    def place(i, j):
        return j == ((((i >> 1) & 15) * 32 + (i >> 5) * 2 + (i & 1) + 32 * ((z + 12) % NZ)) & (KVL - 1))

    perm[...] = spread(KVL, KVL, place)
    pick[...] = spread(2 * NZ * HPD, 128, lambda i, j: j == 32 * (me % 4) + (i >> 3))
    widen[...] = spread(128, 128 * HPD, lambda i, j: (j >> 3) == i)
    pl.semaphore_wait(barrier, len(REACH) + 15 + 2)

    def piece(d):
        return share.at[:, (z + d + 2 * NZ) % NZ]

    def key_piece(d):
        return share.at[:, (z + d + 2 * NZ) % NZ, :, key]

    up = remote(piece(8 - x), relay_v.at[1], vs.at[3], vq.at[1], zdev(4))
    down = remote(piece(-4 - x), relay_v.at[0], vs.at[2], vq.at[0], zdev(-4))
    ahead = remote(piece(4 - x), w.at[0, x, y, pair], vs.at[0], vr.at[0], zdev(4 - x))
    behind = remote(piece(-x), w.at[1, x, y, pair], vs.at[1], vr.at[1], zdev(-x))
    behind_own = local(piece(0), w.at[1, x, y, pair], vr.at[1])
    up.start()
    down.start()
    ahead.start()

    @pl.when(x > 0)
    def _():
        behind.start()

    @pl.when(x == 0)
    def _():
        behind_own.start()

    for n, d in enumerate(FAR_D):
        remote(key_piece(d), relay_k.at[n], zs, zr, zdev(4 if d > 0 else -4)).start()
    for d in REACH:
        remote(key_piece(d), zkeys.at[(4 - d) % NZ], zs, zn, zdev(d)).start()

    for dl, dc in ((0, 1), (1, 0), (1, 1)):
        to = dev(z, 2 * m + (ylo + dl) % 2, (c + dc) % 2)
        remote(qv.at[:, pl.ds(0, NOPE)], qall.at[s], qs, qr, to).start()

    up_rest = remote(relay_v.at[1], w.at[3, x, y, pair], vs.at[5], vr.at[3], zdev(4 - x))
    down_rest = remote(relay_v.at[0], w.at[2, x, y, pair], vs.at[4], vr.at[2], zdev(-x))
    down_own = local(relay_v.at[0], w.at[2, x, y, pair], vr.at[2])

    def forward_far():
        up.wait_recv()
        up_rest.start()
        down.wait_recv()

        @pl.when(x > 0)
        def _():
            down_rest.start()

        @pl.when(x == 0)
        def _():
            down_own.start()

    def forward_keys():
        wait_all(zr, relay_k)
        for n, d in enumerate(FAR_D):
            rest = d - 4 if d > 0 else d + 4
            remote(relay_k.at[n], zkeys.at[(4 - d) % NZ], fs, zf, zdev(rest)).start()

    def chunk(g, src):
        return w.at[pl.ds(2 * g, 2), x, src, pair]

    def to_y(g):
        for n in (4, 3, 5, 2, 6, 1, 7):
            remote(chunk(g, y), chunk(g, y), ys.at[g], yr.at[g, n], dev(z, (y + n) % NY, c)).start()

    def near_ready():
        ahead.wait_recv()
        behind.wait_recv()
        to_y(NEAR)

    def far_ready():
        up_rest.wait_recv()
        down_rest.wait_recv()
        to_y(FAR)

    def all_keys():
        wait_all(zf, relay_k)
        wait_all(zn, zkeys.at[pl.ds(0, 8)])
        own_k.wait()

    def part(g, n, b):
        return w.at[pl.ds(2 * g, 2), b, (y - n + NY) % NY, pair]

    def send_x(g, *ns):
        for n in ns:
            if n:
                wait_all(yr.at[g, n], chunk(g, y))
            ref = part(g, n, x)
            remote(ref, ref, xs.at[g], xf.at[g, n], xdev(sg)).start()
            remote(ref, ref, xs.at[g], xb.at[g], xdev(-sg)).start()

    def relay_x(g, *ns):
        for n in ns:
            ref = part(g, n, (x - sg + NX) % NX)
            cp = remote(ref, ref, xs.at[g], xf.at[g, n], xdev(sg))
            cp.wait_recv()
            remote(ref, ref, xs.at[g], xq.at[g], xdev(sg)).start()

    def to_core(g, b):
        ref = w.at[pl.ds(2 * g, 2), b, :, pair]
        remote(ref, ref, cs, cr, dev(z, y, 1 - c)).start()

    def behind_x(g):
        to_core(g, (x - sg + NX) % NX)

    def other_x(g):
        wait_all(xb.at[g], w.at[0, 0])
        to_core(g, (x + sg + NX) % NX)

    def across_x(g):
        wait_all(xq.at[g], w.at[0, 0])
        to_core(g, (x + 2) % NX)

    def absorb():
        wait_all(qr, qall.at[pl.ds(0, 3)])
        own_q.wait()
        keys = zkeys[...].astype(jnp.float32).reshape(2 * NZ * HPD, NOPE)
        ask = qall[...].astype(jnp.float32).reshape(4 * HPD, NOPE)
        cross = lax.dot_general(
            ask.astype(jnp.bfloat16), keys.astype(jnp.bfloat16), (((1,), (1,)), ((), ())),
            preferred_element_type=jnp.float32,
        )
        r = lax.broadcasted_iota(jnp.int32, cross.shape, 0)
        cc = lax.broadcasted_iota(jnp.int32, cross.shape, 1)
        own = jnp.where((r & (HPD - 1)) == (cc & (HPD - 1)), cross, 0.0).astype(jnp.bfloat16)
        packed = jnp.dot(own, pick[...], preferred_element_type=jnp.float32)
        ab_send[...] = packed.reshape(4, HPD, 128).astype(jnp.bfloat16)
        own_ab.start()
        for n in (8, 9, 7, 10, 6, 11, 5, 12, 4, 13, 3, 14, 2, 15, 1):
            yy, cc2 = (y + n // 2) % NY, (c + n % 2) % 2
            remote(ab_send.at[2 * (yy % 2) + cc2], ab_recv.at[me], a_s, a_r, dev(z, yy, cc2)).start()

    own_ab = local(ab_send.at[s], ab_recv.at[me], loc.at[6])

    def attend():
        fetch_kt.wait()
        fetch_l.wait()
        own_ab.wait()
        wait_all(a_r, ab_recv.at[pl.ds(0, 15)])
        tiles = [sum(ab_recv[4 * g + j].astype(jnp.float32) for j in range(4)) for g in range(4)]
        got = jnp.concatenate(tiles, axis=1).astype(jnp.bfloat16)
        absorbed = jnp.dot(got, perm[...], preferred_element_type=jnp.float32).astype(jnp.bfloat16)
        scores = jnp.dot(absorbed, kt[0:KVL, :], preferred_element_type=jnp.float32)
        scores += jnp.dot(qv[:, NOPE : NOPE + ROPE], kt[KVL : KVL + ROPE, :], preferred_element_type=jnp.float32)
        scores = scores * ((NOPE + ROPE) ** (-0.5))
        count = kt.shape[1]
        positions = m * count + lax.broadcasted_iota(jnp.int32, scores.shape, 1)
        valid = positions < lens[0]
        masked = jnp.where(valid, scores, -1e30)
        top = jnp.max(masked, axis=1, keepdims=True)
        expd = jnp.where(valid, jnp.exp(masked - top), 0.0)
        total = jnp.sum(expd, axis=1, keepdims=True)
        part = lax.dot_general(
            expd.astype(jnp.bfloat16), kt[0:KVL, :], (((1,), (1,)), ((), ())),
            preferred_element_type=jnp.float32,
        )
        lane = lax.broadcasted_iota(jnp.int32, (HPD, 128), 1)
        mg_send[:, 0:KVL] = part
        mg_send[:, KVL : KVL + 128] = jnp.where(lane < 64, top, total)
        for n in (2, 1, 3):
            to = dev(z, (y + 2 * n) % NY, c)
            remote(mg_send, mg_recv.at[n - 1], m_s, m_r, to).start()

    def merge():
        wait_all(m_r, mg_recv)
        parts = [mg_send[...]] + [mg_recv[n] for n in range(3)]
        tops = [p[:, KVL : KVL + 1] for p in parts]
        totals = [p[:, KVL + 64 : KVL + 65] for p in parts]
        top = jnp.maximum(jnp.maximum(tops[0], tops[1]), jnp.maximum(tops[2], tops[3]))
        factors = [jnp.exp(t - top) for t in tops]
        total = sum(f * t for f, t in zip(factors, totals))
        value = sum(f * p[:, 0:KVL] for f, p in zip(factors, parts))
        value = value / total
        high = value.astype(jnp.bfloat16).astype(jnp.float32)
        both = jnp.concatenate([high, value - high], axis=0).astype(jnp.bfloat16)
        r = lax.broadcasted_iota(jnp.int32, (2 * HPD, 128 * HPD), 0)
        cc = lax.broadcasted_iota(jnp.int32, (2 * HPD, 128 * HPD), 1)
        diagonal = (r & (HPD - 1)) == (cc & (HPD - 1))
        for g in range(4):
            wider = jnp.dot(both[:, g * 128 : (g + 1) * 128], widen[...], preferred_element_type=jnp.float32)
            wide[g] = jnp.where(diagonal, wider, 0.0).astype(jnp.bfloat16)

    forward_far()
    near_ready()
    send_x(NEAR, 0)
    forward_keys()
    send_x(NEAR, 1, 7, 2, 6)
    far_ready()
    send_x(FAR, 0)
    all_keys()
    absorb()
    send_x(NEAR, 3, 5, 4)
    relay_x(NEAR, 0, 1, 7, 2, 6)
    to_core(NEAR, x)
    send_x(FAR, 1, 7, 2, 6)
    relay_x(NEAR, 3, 5, 4)
    attend()
    send_x(FAR, 3, 5, 4)
    relay_x(FAR, 0, 1, 7, 2, 6)
    to_core(FAR, x)
    behind_x(NEAR)
    other_x(NEAR)
    across_x(NEAR)
    relay_x(FAR, 3, 5, 4)
    behind_x(FAR)
    other_x(FAR)
    merge()
    across_x(FAR)
    wait_all(cr, w.at[pl.ds(0, 2)])

    wait_all(zs, zkeys.at[pl.ds(0, 15)])
    wait_all(fs, relay_k)
    for cp in (up, down, ahead, up_rest):
        cp.wait_send()

    @pl.when(x > 0)
    def _():
        behind.wait_send()
        down_rest.wait_send()

    wait_all(qs, qall.at[pl.ds(0, 3)])
    for g in (NEAR, FAR):
        wait_all(ys.at[g], w.at[0, 0, pl.ds(0, 7)])
        wait_all(xs.at[g], w.at[0, pl.ds(0, 3)])
    wait_all(cs, w.at[pl.ds(0, 2)])
    wait_all(a_s, ab_recv.at[pl.ds(0, 15)])
    wait_all(m_s, mg_recv)


def project_kernel(w, wide, out, attn, sems):
    z = lax.axis_index("dp")
    copies = []
    for i in range(NZ):
        slot = (i - z + 4 + NZ) % NZ
        cp = pltpu.make_async_copy(w.at[slot // 4, slot % 4], out.at[i], sems.at[i])
        cp.start()
        copies.append(cp)
    total = jnp.zeros((2 * HPD, VDIM), jnp.float32)
    for i in range(NZ):
        slot = (i - z + 4 + NZ) % NZ
        vals = w[slot // 4, slot % 4, :, :, :, NOPE:WIDTH].reshape(32 * HPD, VDIM)
        total += jnp.dot(wide[i // 4, :, (i % 4) * 256 : (i % 4 + 1) * 256], vals, preferred_element_type=jnp.float32)
    attn[0] = (total[0:HPD] + total[HPD:]).astype(jnp.bfloat16)
    for cp in copies:
        cp.wait()


def per_device(kv_weight, queries, kv_cache, lengths):
    rows = kv_weight.shape[0]
    kvw = kv_weight.reshape(rows, NZ, HPD, WIDTH)
    kth = jnp.swapaxes(kv_cache, 1, 2)
    count = kth.shape[2]
    dma = pltpu.SemaphoreType.DMA
    bf16, f32 = jnp.bfloat16, jnp.float32
    vmem = pl.BlockSpec(memory_space=pltpu.VMEM)
    hbm = pl.BlockSpec(memory_space=pltpu.HBM)
    shape = (4, 4, NY, 4, HPD, WIDTH)
    w, wide = pl.pallas_call(
        gather_kernel,
        out_shape=(pltpu.VMEM(shape, bf16), pltpu.VMEM((4, 2 * HPD, 128 * HPD), bf16)),
        in_specs=[hbm, hbm, hbm, hbm],
        out_specs=(vmem, vmem),
        scratch_shapes=[
            pltpu.VMEM((KVL, KVL), bf16),
            pltpu.VMEM((2 * NZ * HPD, 128), bf16),
            pltpu.VMEM((128, 128 * HPD), bf16),
            pltpu.VMEM((2, NZ, HPD, WIDTH), bf16),
            pltpu.VMEM((NZ, 2, HPD, NOPE), bf16),
            pltpu.VMEM((7, 2, HPD, NOPE), bf16),
            pltpu.VMEM((2, 2, HPD, WIDTH), bf16),
            pltpu.VMEM((KVL + ROPE, count), bf16),
            pltpu.VMEM((HPD, NOPE + ROPE), bf16),
            pltpu.SMEM((1,), jnp.int32),
            pltpu.VMEM((4, HPD, NOPE), bf16),
            pltpu.VMEM((4, HPD, 128), bf16),
            pltpu.VMEM((16, HPD, 128), bf16),
            pltpu.VMEM((HPD, KVL + 128), f32),
            pltpu.VMEM((3, HPD, KVL + 128), f32),
            dma((7,)), dma, dma, dma, dma, dma, dma((6,)), dma((4,)), dma((2,)), dma, dma,
            dma((2,)), dma((2, 8)), dma((2,)), dma((2, 8)), dma((2,)), dma((2,)), dma, dma, dma, dma, dma, dma,
        ],
        compiler_params=pltpu.CompilerParams(collective_id=0, has_side_effects=True),
        name="gather",
    )(kvw, queries, kth, lengths)
    w = pltpu.with_memory_space_constraint(w, pltpu.VMEM)
    wide = pltpu.with_memory_space_constraint(wide, pltpu.VMEM)
    out, attn = pl.pallas_call(
        project_kernel,
        out_shape=(jax.ShapeDtypeStruct((NZ, NY, 4, HPD, WIDTH), bf16), jax.ShapeDtypeStruct((1, HPD, VDIM), bf16)),
        in_specs=[vmem, vmem],
        out_specs=(hbm, vmem),
        scratch_shapes=[dma((NZ,))],
        name="project",
    )(w, wide)
    return out.reshape(KVL, HPD, WIDTH), attn


def solution(mesh):
    in_specs = (P(("dp", "mp"), None, None), P("rep", "dp", None), P("rep", "mp", None), P("rep"))
    out_specs = (P(None, "dp", None), P("rep", "dp", None))
    return jax.shard_map(per_device, mesh=mesh, in_specs=in_specs, out_specs=out_specs, check_vma=False)
```

```python
import functools

import jax
import jax.numpy as jnp
from jax import lax
from jax.experimental import pallas as pl
from jax.experimental.pallas import tpu as pltpu
from jax.sharding import PartitionSpec as P

KVL = 512
NOPE = 128
ROPE = 64
VDIM = 128
WIDTH = NOPE + VDIM
NX = 4
NY = 8
NZ = 16
HPD = 8
MESH = pl.DeviceIdType.MESH

NEAR, FAR = 0, 1
REACH = (4, -4, 3, -3, 2, -2, 1, -1)
FAR_D = (8, 7, -7, 6, -6, 5, -5)


def spread(rows, cols, test):
    r = lax.broadcasted_iota(jnp.int32, (rows, cols), 0)
    c = lax.broadcasted_iota(jnp.int32, (rows, cols), 1)
    return jnp.where(test(r, c), 1.0, 0.0).astype(jnp.bfloat16)


def gather_kernel(
    kvw, qh, kth, lenh, w, wide,
    perm, pick, widen, share, zkeys, relay_k, relay_v, kt, qv, lens, qall, ab_send, ab_recv, mg_send, mg_recv,
    loc, zs, zn, zr, zf, fs, vs, vr, vq, qs, qr, ys, yr, xs, xf, xb, xq, cs, cr, a_s, a_r, m_s, m_r,
):
    z = lax.axis_index("dp")
    k = lax.axis_index("rep")
    m = lax.axis_index("mp")
    x = k // 4
    ylo = (k // 2) % 2
    c = k % 2
    y = 2 * m + ylo
    s = 2 * ylo + c
    me = 2 * y + c
    sg = 1 - 2 * c
    key = pl.ds(0, NOPE)
    pair = pl.ds(2 * c, 2)

    def dev(zz, yy, cc, xx=x):
        return {"dp": zz, "rep": xx * 4 + (yy % 2) * 2 + cc, "mp": yy // 2}

    def zdev(d):
        return dev((z + d + 2 * NZ) % NZ, y, c)

    def xdev(d):
        return dev(z, y, c, (x + d + NX) % NX)

    def remote(src, dst, send, recv, to):
        return pltpu.make_async_remote_copy(
            src_ref=src, dst_ref=dst, send_sem=send, recv_sem=recv, device_id=to, device_id_type=MESH
        )

    def local(src, dst, sem):
        return pltpu.make_async_copy(src, dst, sem)

    def wait_all(sem, ref):
        local(ref, ref, sem).wait()

    fetch_w = local(kvw.at[pl.ds(2 * s, 2)], share, loc.at[0])
    fetch_kt = local(kth.at[0], kt, loc.at[1])
    fetch_q = local(qh.at[0], qv, loc.at[2])
    fetch_l = local(lenh, lens, loc.at[3])
    fetch_w.start()
    fetch_q.start()

    barrier = pltpu.get_barrier_semaphore()
    for d in REACH:
        pl.semaphore_signal(barrier, inc=1, device_id=zdev(d), device_id_type=MESH)
    for n in range(1, 2 * NY):
        to = dev(z, (y + n // 2) % NY, (c + n % 2) % 2)
        pl.semaphore_signal(barrier, inc=1, device_id=to, device_id_type=MESH)
    for d in (1, -1):
        pl.semaphore_signal(barrier, inc=1, device_id=xdev(d), device_id_type=MESH)
    fetch_kt.start()
    fetch_l.start()
    fetch_w.wait()
    fetch_q.wait()
    own_q = local(qh.at[0, :, pl.ds(0, NOPE)], qall.at[s], loc.at[4])
    own_q.start()
    own_k = local(share.at[:, z, :, key], zkeys.at[4], loc.at[5])
    own_k.start()

    def place(i, j):
        return j == ((((i >> 1) & 15) * 32 + (i >> 5) * 2 + (i & 1) + 32 * ((z + 12) % NZ)) & (KVL - 1))

    perm[...] = spread(KVL, KVL, place)
    pick[...] = spread(2 * NZ * HPD, 128, lambda i, j: j == 32 * (me % 4) + (i >> 3))
    widen[...] = spread(128, 128 * HPD, lambda i, j: (j >> 3) == i)
    pl.semaphore_wait(barrier, len(REACH) + 15 + 2)

    def piece(d):
        return share.at[:, (z + d + 2 * NZ) % NZ]

    def key_piece(d):
        return share.at[:, (z + d + 2 * NZ) % NZ, :, key]

    up = remote(piece(8 - x), relay_v.at[1], vs.at[3], vq.at[1], zdev(4))
    down = remote(piece(-4 - x), relay_v.at[0], vs.at[2], vq.at[0], zdev(-4))
    ahead = remote(piece(4 - x), w.at[0, x, y, pair], vs.at[0], vr.at[0], zdev(4 - x))
    behind = remote(piece(-x), w.at[1, x, y, pair], vs.at[1], vr.at[1], zdev(-x))
    behind_own = local(piece(0), w.at[1, x, y, pair], vr.at[1])
    up.start()
    down.start()
    ahead.start()

    @pl.when(x > 0)
    def _():
        behind.start()

    @pl.when(x == 0)
    def _():
        behind_own.start()

    for n, d in enumerate(FAR_D):
        remote(key_piece(d), relay_k.at[n], zs, zr, zdev(4 if d > 0 else -4)).start()
    for d in REACH:
        remote(key_piece(d), zkeys.at[(4 - d) % NZ], zs, zn, zdev(d)).start()

    for dl, dc in ((0, 1), (1, 0), (1, 1)):
        to = dev(z, 2 * m + (ylo + dl) % 2, (c + dc) % 2)
        remote(qv.at[:, pl.ds(0, NOPE)], qall.at[s], qs, qr, to).start()

    up_rest = remote(relay_v.at[1], w.at[3, x, y, pair], vs.at[5], vr.at[3], zdev(4 - x))
    down_rest = remote(relay_v.at[0], w.at[2, x, y, pair], vs.at[4], vr.at[2], zdev(-x))
    down_own = local(relay_v.at[0], w.at[2, x, y, pair], vr.at[2])

    def forward_far():
        up.wait_recv()
        up_rest.start()
        down.wait_recv()

        @pl.when(x > 0)
        def _():
            down_rest.start()

        @pl.when(x == 0)
        def _():
            down_own.start()

    def forward_keys():
        wait_all(zr, relay_k)
        for n, d in enumerate(FAR_D):
            rest = d - 4 if d > 0 else d + 4
            remote(relay_k.at[n], zkeys.at[(4 - d) % NZ], fs, zf, zdev(rest)).start()

    def chunk(g, src):
        return w.at[pl.ds(2 * g, 2), x, src, pair]

    def to_y(g):
        for n in (4, 3, 5, 2, 6, 1, 7):
            remote(chunk(g, y), chunk(g, y), ys.at[g], yr.at[g, n], dev(z, (y + n) % NY, c)).start()

    def near_ready():
        ahead.wait_recv()
        behind.wait_recv()
        to_y(NEAR)

    def far_ready():
        up_rest.wait_recv()
        down_rest.wait_recv()
        to_y(FAR)

    def all_keys():
        wait_all(zf, relay_k)
        wait_all(zn, zkeys.at[pl.ds(0, 8)])
        own_k.wait()

    def part(g, n, b):
        return w.at[pl.ds(2 * g, 2), b, (y - n + NY) % NY, pair]

    def send_x(g, *ns):
        for n in ns:
            if n:
                wait_all(yr.at[g, n], chunk(g, y))
            ref = part(g, n, x)
            remote(ref, ref, xs.at[g], xf.at[g, n], xdev(sg)).start()
            remote(ref, ref, xs.at[g], xb.at[g], xdev(-sg)).start()

    def relay_x(g, *ns):
        for n in ns:
            ref = part(g, n, (x - sg + NX) % NX)
            cp = remote(ref, ref, xs.at[g], xf.at[g, n], xdev(sg))
            cp.wait_recv()
            remote(ref, ref, xs.at[g], xq.at[g], xdev(sg)).start()

    def to_core(g, b):
        ref = w.at[pl.ds(2 * g, 2), b, :, pair]
        remote(ref, ref, cs, cr, dev(z, y, 1 - c)).start()

    def behind_x(g):
        to_core(g, (x - sg + NX) % NX)

    def other_x(g):
        wait_all(xb.at[g], w.at[0, 0])
        to_core(g, (x + sg + NX) % NX)

    def across_x(g):
        wait_all(xq.at[g], w.at[0, 0])
        to_core(g, (x + 2) % NX)

    def absorb():
        wait_all(qr, qall.at[pl.ds(0, 3)])
        own_q.wait()
        keys = zkeys[...].astype(jnp.float32).reshape(2 * NZ * HPD, NOPE)
        ask = qall[...].astype(jnp.float32).reshape(4 * HPD, NOPE)
        cross = lax.dot_general(
            ask.astype(jnp.bfloat16), keys.astype(jnp.bfloat16), (((1,), (1,)), ((), ())),
            preferred_element_type=jnp.float32,
        )
        r = lax.broadcasted_iota(jnp.int32, cross.shape, 0)
        cc = lax.broadcasted_iota(jnp.int32, cross.shape, 1)
        own = jnp.where((r & (HPD - 1)) == (cc & (HPD - 1)), cross, 0.0).astype(jnp.bfloat16)
        packed = jnp.dot(own, pick[...], preferred_element_type=jnp.float32)
        ab_send[...] = packed.reshape(4, HPD, 128).astype(jnp.bfloat16)
        own_ab.start()
        for n in (8, 9, 7, 10, 6, 11, 5, 12, 4, 13, 3, 14, 2, 15, 1):
            yy, cc2 = (y + n // 2) % NY, (c + n % 2) % 2
            remote(ab_send.at[2 * (yy % 2) + cc2], ab_recv.at[me], a_s, a_r, dev(z, yy, cc2)).start()

    own_ab = local(ab_send.at[s], ab_recv.at[me], loc.at[6])

    def attend():
        fetch_kt.wait()
        fetch_l.wait()
        own_ab.wait()
        wait_all(a_r, ab_recv.at[pl.ds(0, 15)])
        tiles = [sum(ab_recv[4 * g + j].astype(jnp.float32) for j in range(4)) for g in range(4)]
        got = jnp.concatenate(tiles, axis=1).astype(jnp.bfloat16)
        absorbed = jnp.dot(got, perm[...], preferred_element_type=jnp.float32).astype(jnp.bfloat16)
        scores = jnp.dot(absorbed, kt[0:KVL, :], preferred_element_type=jnp.float32)
        scores += jnp.dot(qv[:, NOPE : NOPE + ROPE], kt[KVL : KVL + ROPE, :], preferred_element_type=jnp.float32)
        scores = scores * ((NOPE + ROPE) ** (-0.5))
        count = kt.shape[1]
        positions = m * count + lax.broadcasted_iota(jnp.int32, scores.shape, 1)
        valid = positions < lens[0]
        masked = jnp.where(valid, scores, -1e30)
        top = jnp.max(masked, axis=1, keepdims=True)
        expd = jnp.where(valid, jnp.exp(masked - top), 0.0)
        total = jnp.sum(expd, axis=1, keepdims=True)
        part = lax.dot_general(
            expd.astype(jnp.bfloat16), kt[0:KVL, :], (((1,), (1,)), ((), ())),
            preferred_element_type=jnp.float32,
        )
        lane = lax.broadcasted_iota(jnp.int32, (HPD, 128), 1)
        mg_send[:, 0:KVL] = part
        mg_send[:, KVL : KVL + 128] = jnp.where(lane < 64, top, total)
        for n in (2, 1, 3):
            to = dev(z, (y + 2 * n) % NY, c)
            remote(mg_send, mg_recv.at[n - 1], m_s, m_r, to).start()

    def merge():
        wait_all(m_r, mg_recv)
        parts = [mg_send[...]] + [mg_recv[n] for n in range(3)]
        tops = [p[:, KVL : KVL + 1] for p in parts]
        totals = [p[:, KVL + 64 : KVL + 65] for p in parts]
        top = jnp.maximum(jnp.maximum(tops[0], tops[1]), jnp.maximum(tops[2], tops[3]))
        factors = [jnp.exp(t - top) for t in tops]
        total = sum(f * t for f, t in zip(factors, totals))
        value = sum(f * p[:, 0:KVL] for f, p in zip(factors, parts))
        value = value / total
        high = value.astype(jnp.bfloat16).astype(jnp.float32)
        both = jnp.concatenate([high, value - high], axis=0).astype(jnp.bfloat16)
        r = lax.broadcasted_iota(jnp.int32, (2 * HPD, 128 * HPD), 0)
        cc = lax.broadcasted_iota(jnp.int32, (2 * HPD, 128 * HPD), 1)
        diagonal = (r & (HPD - 1)) == (cc & (HPD - 1))
        for g in range(4):
            wider = jnp.dot(both[:, g * 128 : (g + 1) * 128], widen[...], preferred_element_type=jnp.float32)
            wide[g] = jnp.where(diagonal, wider, 0.0).astype(jnp.bfloat16)

    forward_far()
    near_ready()
    send_x(NEAR, 0)
    forward_keys()
    send_x(NEAR, 1, 7, 2, 6)
    far_ready()
    send_x(FAR, 0)
    all_keys()
    absorb()
    send_x(NEAR, 3, 5, 4)
    to_core(NEAR, x)
    send_x(FAR, 1, 7, 2, 6, 3, 5, 4)
    to_core(FAR, x)
    attend()
    relay_x(NEAR, 0, 1, 7, 2, 6, 3, 5, 4)
    behind_x(NEAR)
    relay_x(FAR, 0, 1, 7, 2, 6, 3, 5, 4)
    behind_x(FAR)
    other_x(NEAR)
    other_x(FAR)
    across_x(NEAR)
    merge()
    across_x(FAR)
    wait_all(cr, w.at[pl.ds(0, 2)])

    wait_all(zs, zkeys.at[pl.ds(0, 15)])
    wait_all(fs, relay_k)
    for cp in (up, down, ahead, up_rest):
        cp.wait_send()

    @pl.when(x > 0)
    def _():
        behind.wait_send()
        down_rest.wait_send()

    wait_all(qs, qall.at[pl.ds(0, 3)])
    for g in (NEAR, FAR):
        wait_all(ys.at[g], w.at[0, 0, pl.ds(0, 7)])
        wait_all(xs.at[g], w.at[0, pl.ds(0, 3)])
    wait_all(cs, w.at[pl.ds(0, 2)])
    wait_all(a_s, ab_recv.at[pl.ds(0, 15)])
    wait_all(m_s, mg_recv)


def project_kernel(w, wide, out, attn, sems):
    z = lax.axis_index("dp")
    copies = []
    for i in range(NZ):
        slot = (i - z + 4 + NZ) % NZ
        cp = pltpu.make_async_copy(w.at[slot // 4, slot % 4], out.at[i], sems.at[i])
        cp.start()
        copies.append(cp)
    total = jnp.zeros((2 * HPD, VDIM), jnp.float32)
    for i in range(NZ):
        slot = (i - z + 4 + NZ) % NZ
        vals = w[slot // 4, slot % 4, :, :, :, NOPE:WIDTH].reshape(32 * HPD, VDIM)
        total += jnp.dot(wide[i // 4, :, (i % 4) * 256 : (i % 4 + 1) * 256], vals, preferred_element_type=jnp.float32)
    attn[0] = (total[0:HPD] + total[HPD:]).astype(jnp.bfloat16)
    for cp in copies:
        cp.wait()


def per_device(kv_weight, queries, kv_cache, lengths):
    rows = kv_weight.shape[0]
    kvw = kv_weight.reshape(rows, NZ, HPD, WIDTH)
    kth = jnp.swapaxes(kv_cache, 1, 2)
    count = kth.shape[2]
    dma = pltpu.SemaphoreType.DMA
    bf16, f32 = jnp.bfloat16, jnp.float32
    vmem = pl.BlockSpec(memory_space=pltpu.VMEM)
    hbm = pl.BlockSpec(memory_space=pltpu.HBM)
    shape = (4, 4, NY, 4, HPD, WIDTH)
    w, wide = pl.pallas_call(
        gather_kernel,
        out_shape=(pltpu.VMEM(shape, bf16), pltpu.VMEM((4, 2 * HPD, 128 * HPD), bf16)),
        in_specs=[hbm, hbm, hbm, hbm],
        out_specs=(vmem, vmem),
        scratch_shapes=[
            pltpu.VMEM((KVL, KVL), bf16),
            pltpu.VMEM((2 * NZ * HPD, 128), bf16),
            pltpu.VMEM((128, 128 * HPD), bf16),
            pltpu.VMEM((2, NZ, HPD, WIDTH), bf16),
            pltpu.VMEM((NZ, 2, HPD, NOPE), bf16),
            pltpu.VMEM((7, 2, HPD, NOPE), bf16),
            pltpu.VMEM((2, 2, HPD, WIDTH), bf16),
            pltpu.VMEM((KVL + ROPE, count), bf16),
            pltpu.VMEM((HPD, NOPE + ROPE), bf16),
            pltpu.SMEM((1,), jnp.int32),
            pltpu.VMEM((4, HPD, NOPE), bf16),
            pltpu.VMEM((4, HPD, 128), bf16),
            pltpu.VMEM((16, HPD, 128), bf16),
            pltpu.VMEM((HPD, KVL + 128), f32),
            pltpu.VMEM((3, HPD, KVL + 128), f32),
            dma((7,)), dma, dma, dma, dma, dma, dma((6,)), dma((4,)), dma((2,)), dma, dma,
            dma((2,)), dma((2, 8)), dma((2,)), dma((2, 8)), dma((2,)), dma((2,)), dma, dma, dma, dma, dma, dma,
        ],
        compiler_params=pltpu.CompilerParams(collective_id=0, has_side_effects=True),
        name="gather",
    )(kvw, queries, kth, lengths)
    w = pltpu.with_memory_space_constraint(w, pltpu.VMEM)
    wide = pltpu.with_memory_space_constraint(wide, pltpu.VMEM)
    out, attn = pl.pallas_call(
        project_kernel,
        out_shape=(jax.ShapeDtypeStruct((NZ, NY, 4, HPD, WIDTH), bf16), jax.ShapeDtypeStruct((1, HPD, VDIM), bf16)),
        in_specs=[vmem, vmem],
        out_specs=(hbm, vmem),
        scratch_shapes=[dma((NZ,))],
        name="project",
    )(w, wide)
    return out.reshape(KVL, HPD, WIDTH), attn


def solution(mesh):
    in_specs = (P(("dp", "mp"), None, None), P("rep", "dp", None), P("rep", "mp", None), P("rep"))
    out_specs = (P(None, "dp", None), P("rep", "dp", None))
    return jax.shard_map(per_device, mesh=mesh, in_specs=in_specs, out_specs=out_specs, check_vma=False)
```
